32 devices in a mesh: group: 2 (over y), swap: 8 (over z, x), image: 2 (over core).
Axes of the slice: x: 2, y: 2, z: 4, core: 2. Of those that a mesh axis runs over, the one named last changes fastest.
Arguments:
- images_in: bfloat16 [16, 1536, 4096], P(('group', 'image'), 'swap'), parts along dimension 0, may hold values from -6 to 6
- kernel: bfloat16 [1536, 49], P('swap'), may hold values from -1.75 to 1.75
- conv_bias: float32 [1536], P('swap'), may hold values from -1 to 1
- norm_gain: float32 [1536], replicated, may hold values from 0.1 to 1.9
- norm_shift: float32 [1536], replicated, may hold values from -0.5 to 0.5
- fp8_weight: bfloat16 [1536, 6144], P('swap', 'image'), may hold values from -1.875 to 1.875, as said below
- block_scale: int32 [1536, 48], P('swap', 'image'), may hold values from -7 to -5
- adapter_a: bfloat16 [1536, 32], replicated, may hold values from -0.15625 to 0.15625
- adapter_b: bfloat16 [32, 6144], P(None, 'image'), may hold values from -0.25 to 0.25
- cotangent: bfloat16 [16, 4096, 6144], P('group', 'swap', 'image'), parts along dimension 0, may hold values from -0.05 to 0.05
Outputs:
- grad_a: float32 [3072, 32], P('group'), parts along dimension 0
- grad_b: float32 [64, 6144], P('group', 'image'), parts along dimension 0
The draws below stay inside these ranges and needn't reach their ends.
There are 2 independent parts, one for each index of `group`. The reference program is written for one: setup_inputs(seed, part) draws one part's arguments, and reference() takes and returns one part's arrays. A program takes and returns all parts, laid end to end along the dimension named above; an argument that names none is the same for every part. Nothing has to cross between parts.
Inputs may be any that keep to these rules, and one draw needn't show every extreme that they name: `fp8_weight`: each entry is a value of the E4M3 format: a sign times 2 to an integer power times 1 + k / 8 for an integer k of 0 to 7. `block_scale`: the entry at [c, j] is the exponent of the scale of hidden units 128 * j to 128 * j + 127 of weight row c.
All inputs are finite; a program needn't handle non-finite values.
Results may differ from the reference program's by a relative error of at most 0.00055.
The reference program's roundings to bfloat16 on the way (of `conv`, `normed`, `scaled_weight`, `low_rank` and `grad_pre`) count: a program that leaves them out, or rounds other values in their place, can miss the bound.
Values may be sent and summed in bfloat16 or wider, within the bound.
A program may use at most 192 MiB of HBM per device.

```python
import math
import jax
import jax.numpy as jnp
from jax import lax

C = 1536
FF = 6144
R = 32
KS = 7
H = 64
W = 64
IMAGES = 8


def draw_kernel(key, part):
    first_key, second_key = jax.random.split(key)
    spread = jnp.exp(jax.random.uniform(second_key, (C, 1), jnp.float32, math.log(0.3), math.log(3.0)))
    values = jnp.clip(jax.random.normal(first_key, (C, KS * KS), jnp.float32), -4.0, 4.0)
    return (values * spread / KS).astype(jnp.bfloat16)


def draw_fp8_weight(key, part):
    sign_key, power_key, mantissa_key = jax.random.split(key, 3)
    lowest = -2
    negative = jax.random.bernoulli(sign_key, 0.5, (C, FF))
    exponent = jax.random.randint(power_key, (C, FF), lowest, 1)
    mantissa = jax.random.randint(mantissa_key, (C, FF), 0, 8)
    power = jnp.where(exponent == -3, 0.125, jnp.where(exponent == -2, 0.25, jnp.where(exponent == -1, 0.5, 1.0)))
    signs = jnp.where(negative, -1.0, 1.0)
    values = signs * power * (1.0 + mantissa.astype(jnp.float32) / 8.0)
    return values.astype(jnp.float32).astype(jnp.bfloat16)


def draw_cotangent(key, part):
    value_key, scale_key = jax.random.split(key, 2)
    shape = (IMAGES, H * W, FF)
    row_scale = jnp.exp(jax.random.uniform(scale_key, (IMAGES, H * W, 1), jnp.float32, 0.0, math.log(10.0)))
    values = jnp.clip(jax.random.normal(value_key, shape, jnp.float32), -4.0, 4.0)
    return (values * row_scale / 1024.0).astype(jnp.bfloat16)


def place_ends(entries, stream_key, least, largest):
    place = [jax.random.randint(jax.random.fold_in(stream_key, axis), (), 0, length) for axis, length in enumerate(entries.shape)]
    main_axis = entries.shape.index(max(entries.shape))
    beside = place[:main_axis] + [(place[main_axis] + 1) % entries.shape[main_axis]] + place[main_axis + 1:]
    return entries.at[tuple(place)].set(least).at[tuple(beside)].set(largest)


def steps_of(stream_key, extent, cuts, least, largest):
    level, own = 1.0, jax.random.fold_in(stream_key, 6)
    for position, shards_of in cuts:
        draws = jnp.exp(jax.random.uniform(jax.random.fold_in(own, position), (shards_of,), jnp.float32, least / len(cuts), largest / len(cuts)))
        level = level * jnp.repeat(draws, extent[position] // shards_of).reshape([-1 if axis == position else 1 for axis in range(len(extent))])
    return level


def noise(rng, dims, width, most, pieces=(), dtype=jnp.bfloat16):
    loudness = steps_of(rng, dims, pieces, -0.22, 0.18) if pieces else 1.0
    result = jax.random.normal(rng, dims, jnp.float32) * width * loudness
    return jnp.minimum(jnp.maximum(result, -most), most).astype(dtype)


def setup_inputs(seed: int = 0, part: int = 0) -> dict:
    key_list = jax.random.split(jax.random.key(seed), 11)
    own_keys = jax.random.split(jax.random.fold_in(key_list[10], part), 11)
    images_in = noise(own_keys[0], (IMAGES, C, H * W), 1.0, 6.0, ((0, 2), (1, 8)))
    kernel = draw_kernel(jax.random.fold_in(key_list[10], 71), part)
    conv_bias = jnp.clip(jax.random.uniform(key_list[2], (C,), jnp.float32, -1.0, 1.0) * steps_of(key_list[2], (C,), ((0, 8),), -0.4, 0.0), -1.0, 1.0)
    norm_gain = jnp.clip(1.0 + 0.18 * jax.random.normal(key_list[3], (C,), jnp.float32), 0.1, 1.9)
    norm_shift = jnp.clip(jax.random.uniform(key_list[4], (C,), jnp.float32, -0.5, 0.5), -0.5, 0.5)
    fp8_weight = draw_fp8_weight(jax.random.fold_in(key_list[10], 71), part)
    block_scale = place_ends(jax.random.randint(key_list[6], (C, FF // 128), -7, -4), jax.random.fold_in(key_list[6], 1), -7, (-4) - 1).astype(jnp.int32)
    adapter_a = noise(key_list[7], (C, R), C ** -0.5, 0.15625)
    adapter_b = noise(key_list[8], (R, FF), (R * 16) ** -0.5, 0.25, ((1, 2),))
    cotangent = draw_cotangent(jax.random.fold_in(jax.random.fold_in(key_list[10], part), 71), part)
    return {"images_in": images_in, "kernel": kernel, "conv_bias": conv_bias, "norm_gain": norm_gain, "norm_shift": norm_shift, "fp8_weight": fp8_weight, "block_scale": block_scale, "adapter_a": adapter_a, "adapter_b": adapter_b, "cotangent": cotangent}


adapter_scale = 2.0
norm_eps = 1e-06

def power_table(scales):
    factor = jnp.zeros(scales.shape, jnp.float32)
    for exponent in range(-12, 4):
        factor = factor + jnp.where(scales == exponent, jnp.float32(2.0 ** exponent), jnp.float32(0.0))
    return factor

def decode(weight, scales):
    row_count = weight.shape[0]
    groups = scales.shape[1]
    blocks = weight.reshape(row_count, groups, -1).astype(jnp.float32) * power_table(scales)[:, :, None]
    return blocks.reshape(row_count, -1).astype(jnp.bfloat16)

def gelu_slope(pre_act):
    cumulative = 0.5 * (1.0 + jax.scipy.special.erf(pre_act * 0.7071067811865476))
    density = jnp.exp(-0.5 * pre_act * pre_act) * 0.3989422804014327
    return cumulative + pre_act * density

def depthwise(images, kernel, conv_bias, map_width):
    pixels = images.shape[-1]
    last_axis = images.ndim - 1
    half_span = KS // 2
    margin = half_span * map_width + half_span
    padded = jnp.pad(images, [(0, 0)] * last_axis + [(margin, margin)])
    column = jnp.arange(pixels) % map_width
    weights = kernel.astype(jnp.float32)
    summed = jnp.zeros(images.shape, jnp.float32)
    for row_step in range(KS):
        for col_step in range(KS):
            offset = (row_step - half_span) * map_width + (col_step - half_span)
            shifted = lax.slice_in_dim(padded, margin + offset, margin + offset + pixels, axis=last_axis)
            moved = column + (col_step - half_span)
            inside = ((moved >= 0) & (moved < map_width)).astype(jnp.float32)
            summed = summed + shifted.astype(jnp.float32) * weights[:, row_step * KS + col_step][:, None] * inside
    return summed + conv_bias.astype(jnp.float32)[:, None]

def reference(images_in, kernel, conv_bias, norm_gain, norm_shift, fp8_weight, block_scale, adapter_a, adapter_b, cotangent):
    scaled_weight = decode(fp8_weight, block_scale)

    def one_image(carry, inputs):
        image, upstream = inputs
        conv = depthwise(image, kernel, conv_bias, W).astype(jnp.bfloat16)
        values = conv.astype(jnp.float32)
        average = lax.optimization_barrier(jnp.mean(values, axis=0, keepdims=True))
        centred = values - average
        variance = lax.optimization_barrier(jnp.mean(centred * centred, axis=0, keepdims=True))
        scaled = centred * lax.rsqrt(variance + norm_eps) * norm_gain[:, None] + norm_shift[:, None]
        normed = scaled.T.astype(jnp.bfloat16)
        low_rank = jnp.dot(normed, adapter_a, preferred_element_type=jnp.float32).astype(jnp.bfloat16)
        pre_act = jnp.dot(normed, scaled_weight, preferred_element_type=jnp.float32)
        pre_act = pre_act + adapter_scale * jnp.dot(low_rank, adapter_b, preferred_element_type=jnp.float32)
        grad_pre = (upstream.astype(jnp.float32) * gelu_slope(pre_act)).astype(jnp.bfloat16)
        grad_b = adapter_scale * jnp.dot(low_rank.T, grad_pre, preferred_element_type=jnp.float32)
        back_low = jnp.dot(grad_pre, adapter_b.T, preferred_element_type=jnp.float32)
        grad_a = adapter_scale * jnp.dot(normed.astype(jnp.float32).T, back_low, precision=lax.Precision.HIGHEST)
        return ((carry[0] + grad_a, carry[1] + grad_b), None)
    initial = (jnp.zeros((C, R), jnp.float32), jnp.zeros((R, FF), jnp.float32))
    totals, unused = lax.scan(one_image, initial, (images_in, cotangent))
    return (totals[0], totals[1])
```

```python
import functools

import jax
import jax.numpy as jnp
from jax import lax
from jax.experimental import pallas as pl
from jax.experimental.pallas import tpu as pltpu
from jax.sharding import PartitionSpec as P

KS = 7
W = 64
HALF = KS // 2
MESH = pl.DeviceIdType.MESH
CH = 16
SPAN = 1024
MARGIN = 256


adapter_scale = 2.0
norm_eps = 1e-06


def power_table(scales):
    factor = jnp.zeros(scales.shape, jnp.float32)
    for exponent in range(-12, 4):
        factor = factor + jnp.where(
            scales == exponent, jnp.float32(2.0**exponent), jnp.float32(0.0)
        )
    return factor


def decode(weight, scales):
    row_count = weight.shape[0]
    groups = scales.shape[1]
    blocks = (
        weight.reshape(row_count, groups, -1).astype(jnp.float32) * power_table(scales)[:, :, None]
    )
    return blocks.reshape(row_count, -1).astype(jnp.bfloat16)


def gelu_slope(pre_act):
    cumulative = 0.5 * (1.0 + lax.erf(pre_act * 0.7071067811865476))
    density = jnp.exp(-0.5 * pre_act * pre_act) * 0.3989422804014327
    return cumulative + pre_act * density


def conv_block(x_ref, k_ref, b_ref, block, shifted, taps, put):
    pixels = x_ref.shape[-1]
    rows = pl.ds(pl.multiple_of(block * CH, CH), CH)
    x = x_ref[rows, :].astype(jnp.float32)
    column = lax.broadcasted_iota(jnp.int32, (CH, pixels), 1) & (W - 1)
    for b in range(KS):
        step = b - HALF
        if step == 0:
            moved = x
        else:
            moved = pltpu.roll(x, (-step) % pixels, axis=1)
            inside = column + step
            moved = jnp.where((inside >= 0) & (inside < W), moved, 0.0)
        shifted[b, :, MARGIN : MARGIN + pixels] = moved
    k = k_ref[rows, :].astype(jnp.float32)
    for t in range(KS * KS):
        taps[t] = jnp.broadcast_to(k[:, t : t + 1], (CH, 128))
    bias = b_ref[rows, :]

    def part(i, carry):
        start = i * SPAN
        even = jnp.broadcast_to(bias, (CH, SPAN))
        odd = jnp.zeros((CH, SPAN + 128), jnp.float32)
        for a in range(KS):
            step = a - HALF
            for b in range(KS):
                tap = taps[a * KS + b]
                if step % 2 == 0:
                    at = pl.ds(pl.multiple_of(start + MARGIN + step * W, 128), SPAN)
                    even = even + shifted[b, :, at] * jnp.tile(tap, (1, SPAN // 128))
                else:
                    at = pl.ds(pl.multiple_of(start + MARGIN + (step - 1) * W, 128), SPAN + 128)
                    odd = odd + shifted[b, :, at] * jnp.tile(tap, (1, SPAN // 128 + 1))
        moved = pltpu.roll(odd, SPAN + 128 - W, axis=1)[:, :SPAN]
        put(i, (even + moved).astype(jnp.bfloat16))
        return carry

    lax.fori_loop(0, pixels // SPAN, part, 0)


def exchange_kernel(
    n,
    x_hbm,
    k_ref,
    b_ref,
    out_hbm,
    x_buf,
    shifted,
    taps,
    stage,
    load_sem,
    own_sem,
    send_sem,
    recv_sem,
    fsend_sem,
    frecv_sem,
):
    images, channels, pixels = x_hbm.shape
    piece = pixels // n
    me = lax.axis_index("swap")
    core = lax.axis_index("image")
    other = 1 - core
    first = core * images
    for i in range(images):
        pltpu.make_async_copy(x_hbm.at[i], x_buf.at[i], load_sem.at[i]).start()
    barrier = pltpu.get_barrier_semaphore()
    for k in range(1, n):
        pl.semaphore_signal(
            barrier, inc=1, device_id={"swap": lax.rem(me + k, n)}, device_id_type=MESH
        )
    pl.semaphore_signal(barrier, inc=1, device_id={"image": other}, device_id_type=MESH)
    shifted[...] = jnp.zeros_like(shifted)
    pl.semaphore_wait(barrier, n)

    my_rows = pl.ds(pl.multiple_of(me * channels, channels), channels)

    def sent(i, k):
        peer = lax.rem(me + k, n)
        return pltpu.make_async_remote_copy(
            src_ref=stage.at[i, peer],
            dst_ref=out_hbm.at[first + i, my_rows],
            send_sem=send_sem.at[i, k],
            recv_sem=recv_sem.at[i, k],
            device_id={"swap": peer},
            device_id_type=MESH,
        )

    def own(i):
        return pltpu.make_async_copy(
            stage.at[i, me], out_hbm.at[first + i, my_rows], own_sem.at[i]
        )

    def forward(i):
        return pltpu.make_async_remote_copy(
            src_ref=out_hbm.at[first + i],
            dst_ref=out_hbm.at[first + i],
            send_sem=fsend_sem.at[i],
            recv_sem=frecv_sem.at[i],
            device_id={"image": other},
            device_id_type=MESH,
        )

    for i in range(images):
        pltpu.make_async_copy(x_hbm.at[i], x_buf.at[i], load_sem.at[i]).wait()

        def one(block, carry):
            rows = pl.ds(pl.multiple_of(block * CH, CH), CH)

            def put(j, values):
                for s in range(SPAN // piece):
                    stage[i, j * (SPAN // piece) + s, rows, :] = values[
                        :, s * piece : (s + 1) * piece
                    ]

            conv_block(x_buf.at[i], k_ref, b_ref, block, shifted, taps, put)
            return carry

        lax.fori_loop(0, channels // CH, one, 0)
        for k in range(1, n):
            sent(i, k).start()
        own(i).start()
    for i in range(images):
        for k in range(1, n):
            sent(i, k).wait_recv()
        own(i).wait()
        forward(i).start()
    for i in range(images):
        forward(i).wait_recv()
    for i in range(images):
        for k in range(1, n):
            sent(i, k).wait_send()
        forward(i).wait_send()


def exchange(n, images_in, kernel, conv_bias):
    images, channels, pixels = images_in.shape
    piece = pixels // n
    dma = pltpu.SemaphoreType.DMA
    return pl.pallas_call(
        functools.partial(exchange_kernel, n),
        out_shape=jax.ShapeDtypeStruct((2 * images, channels * n, piece), jnp.bfloat16),
        in_specs=[
            pl.BlockSpec(memory_space=pltpu.HBM),
            pl.BlockSpec(memory_space=pltpu.VMEM),
            pl.BlockSpec(memory_space=pltpu.VMEM),
        ],
        out_specs=pl.BlockSpec(memory_space=pltpu.HBM),
        scratch_shapes=[
            pltpu.VMEM((images, channels, pixels), jnp.bfloat16),
            pltpu.VMEM((KS, CH, pixels + 2 * MARGIN), jnp.float32),
            pltpu.VMEM((KS * KS, CH, 128), jnp.float32),
            pltpu.VMEM((images, n, channels, piece), jnp.bfloat16),
            dma((images,)),
            dma((images,)),
            dma((images, n)),
            dma((images, n)),
            dma((images,)),
            dma((images,)),
        ],
        compiler_params=pltpu.CompilerParams(
            collective_id=0, has_side_effects=True, vmem_limit_bytes=48 * 2**20
        ),
        cost_estimate=pl.CostEstimate(
            flops=int(2e11), bytes_accessed=int(4e7), transcendentals=0
        ),
        name="conv_exchange",
    )(images_in, kernel, conv_bias)


def main_kernel(x_ref, w_ref, cot_ref, a_ref, b_ref, gain_ref, shift_ref, ga_ref, gb_ref, tok):
    @pl.when(pl.program_id(0) == 0)
    def _():
        ga_ref[...] = jnp.zeros_like(ga_ref)
        gb_ref[...] = jnp.zeros_like(gb_ref)

    channels, piece = x_ref.shape[1:]
    hidden = w_ref.shape[1]
    lanes = 128
    for s in range(piece // lanes):
        at = slice(s * lanes, (s + 1) * lanes)
        x = x_ref[0, :, at].astype(jnp.float32)
        average = jnp.sum(x, axis=0, keepdims=True) * (1.0 / channels)
        centred = x - average
        variance = jnp.sum(centred * centred, axis=0, keepdims=True) * (1.0 / channels)
        scaled = centred * lax.rsqrt(variance + norm_eps) * gain_ref[...] + shift_ref[...]
        tok[at, :] = jnp.swapaxes(scaled, 0, 1).astype(jnp.bfloat16)
    tokens = tok[...]
    low = jnp.dot(tokens, a_ref[...], preferred_element_type=jnp.float32).astype(jnp.bfloat16)
    low_t = jnp.swapaxes(low.astype(jnp.float32), 0, 1).astype(jnp.bfloat16)
    step = 512

    def columns(j, back):
        at = pl.ds(pl.multiple_of(j * step, step), step)
        up = b_ref[:, at]
        pre = jnp.dot(tokens, w_ref[:, at], preferred_element_type=jnp.float32)
        pre = pre + adapter_scale * jnp.dot(low, up, preferred_element_type=jnp.float32)
        grad = (cot_ref[0, :, at].astype(jnp.float32) * gelu_slope(pre)).astype(jnp.bfloat16)
        gb_ref[:, at] += adapter_scale * jnp.dot(low_t, grad, preferred_element_type=jnp.float32)
        return back + lax.dot_general(
            up, grad, (((1,), (1,)), ((), ())), preferred_element_type=jnp.float32
        )

    back = jnp.zeros((b_ref.shape[0], piece), jnp.float32)
    for j in range(hidden // step):
        back = columns(j, back)
    high = back.astype(jnp.bfloat16)
    rest = back - high.astype(jnp.float32)
    middle = rest.astype(jnp.bfloat16)
    least = (rest - middle.astype(jnp.float32)).astype(jnp.bfloat16)
    total = jnp.dot(high, tokens, preferred_element_type=jnp.float32)
    total = total + jnp.dot(middle, tokens, preferred_element_type=jnp.float32)
    total = total + jnp.dot(least, tokens, preferred_element_type=jnp.float32)
    ga_ref[...] += adapter_scale * total


def main_part(conv, weight, cotangent, adapter_a, adapter_b, gain, shift):
    images, channels, piece = conv.shape
    hidden = weight.shape[1]
    rank = adapter_a.shape[1]
    once = lambda shape: pl.BlockSpec(
        shape, lambda i: (0,) * len(shape), pipeline_mode=pl.Buffered(1)
    )
    return pl.pallas_call(
        main_kernel,
        grid=(images,),
        out_shape=(
            jax.ShapeDtypeStruct((rank, channels), jnp.float32),
            jax.ShapeDtypeStruct((rank, hidden), jnp.float32),
        ),
        in_specs=[
            pl.BlockSpec((1, channels, piece), lambda i: (i, 0, 0)),
            once((channels, hidden)),
            pl.BlockSpec((1, piece, hidden), lambda i: (i, 0, 0)),
            once((channels, rank)),
            once((rank, hidden)),
            once((channels, 1)),
            once((channels, 1)),
        ],
        out_specs=(
            pl.BlockSpec((rank, channels), lambda i: (0, 0)),
            pl.BlockSpec((rank, hidden), lambda i: (0, 0)),
        ),
        scratch_shapes=[pltpu.VMEM((piece, channels), jnp.bfloat16)],
        compiler_params=pltpu.CompilerParams(
            dimension_semantics=("arbitrary",), vmem_limit_bytes=56 * 2**20
        ),
        cost_estimate=pl.CostEstimate(
            flops=int(4.4e10), bytes_accessed=int(5e7), transcendentals=int(2.5e7)
        ),
        name="tokens_main",
    )(conv, weight, cotangent, adapter_a, adapter_b, gain[:, None], shift[:, None])


def sum_kernel(n, ga_ref, gb_ref, oa_ref, ob_ref, pair, held, parts, total, pair_sem, s1, r1, s2, r2):
    me = lax.axis_index("swap")
    other = 1 - lax.axis_index("image")
    rank, wide_a = ga_ref.shape
    wide_b = gb_ref.shape[1]
    per = n // (rank // 8)
    ca, cb = wide_a // per, wide_b // per
    barrier = pltpu.get_barrier_semaphore()
    for k in range(1, n):
        pl.semaphore_signal(
            barrier, inc=1, device_id={"swap": lax.rem(me + k, n)}, device_id_type=MESH
        )
    pl.semaphore_signal(barrier, inc=1, device_id={"image": other}, device_id_type=MESH)
    pl.semaphore_wait(barrier, n)
    swap_a = pltpu.make_async_remote_copy(
        src_ref=ga_ref,
        dst_ref=pair,
        send_sem=pair_sem.at[0],
        recv_sem=pair_sem.at[1],
        device_id={"image": other},
        device_id_type=MESH,
    )
    swap_a.start()

    def place(ref, j, width):
        return ref.at[
            pl.ds(pl.multiple_of((j // per) * 8, 8), 8),
            pl.ds(pl.multiple_of((j % per) * width, 128), width),
        ]

    def move(src, dst, peer, ss, rs):
        return pltpu.make_async_remote_copy(
            src_ref=src,
            dst_ref=dst,
            send_sem=ss,
            recv_sem=rs,
            device_id={"swap": peer},
            device_id_type=MESH,
        )

    def scatter_b(k):
        peer = lax.rem(me + k, n)
        return move(
            place(gb_ref, peer, cb), parts.at[k, :, ca : ca + cb], peer, s1.at[1, k], r1.at[1, k]
        )

    def scatter_a(k):
        peer = lax.rem(me + k, n)
        return move(
            place(held, peer, ca), parts.at[k, :, 0:ca], peer, s1.at[0, k], r1.at[0, k]
        )

    for k in range(1, n):
        scatter_b(k).start()
    swap_a.wait()
    held[...] = ga_ref[...] + pair[...]
    for k in range(1, n):
        scatter_a(k).start()
    sum_b = place(gb_ref, me, cb)[...]
    for k in range(1, n):
        scatter_b(k).wait_recv()
        sum_b = sum_b + parts[k, :, ca : ca + cb]
    sum_a = place(held, me, ca)[...]
    for k in range(1, n):
        scatter_a(k).wait_recv()
        sum_a = sum_a + parts[k, :, 0:ca]
    total[:, 0:ca] = sum_a
    total[:, ca : ca + cb] = sum_b
    place(oa_ref, me, ca)[...] = sum_a
    place(ob_ref, me, cb)[...] = sum_b

    def gather_a(k):
        peer = lax.rem(me + k, n)
        return move(total.at[:, 0:ca], place(oa_ref, me, ca), peer, s2.at[0, k], r2.at[0, k])

    def gather_b(k):
        peer = lax.rem(me + k, n)
        return move(
            total.at[:, ca : ca + cb], place(ob_ref, me, cb), peer, s2.at[1, k], r2.at[1, k]
        )

    for k in range(1, n):
        gather_b(k).start()
        gather_a(k).start()
    for k in range(1, n):
        gather_b(k).wait_recv()
        gather_a(k).wait_recv()
    for k in range(1, n):
        scatter_a(k).wait_send()
        scatter_b(k).wait_send()
        gather_a(k).wait_send()
        gather_b(k).wait_send()


def sum_all(n, grad_a, grad_b):
    rank, wide_a = grad_a.shape
    wide_b = grad_b.shape[1]
    per = n // (rank // 8)
    wide = wide_a // per + wide_b // per
    dma = pltpu.SemaphoreType.DMA
    vmem = pl.BlockSpec(memory_space=pltpu.VMEM)
    return pl.pallas_call(
        functools.partial(sum_kernel, n),
        out_shape=(
            jax.ShapeDtypeStruct(grad_a.shape, jnp.float32),
            jax.ShapeDtypeStruct(grad_b.shape, jnp.float32),
        ),
        in_specs=[vmem, vmem],
        out_specs=(vmem, vmem),
        scratch_shapes=[
            pltpu.VMEM(grad_a.shape, jnp.float32),
            pltpu.VMEM(grad_a.shape, jnp.float32),
            pltpu.VMEM((n, 8, wide), jnp.float32),
            pltpu.VMEM((8, wide), jnp.float32),
            dma((2,)),
            dma((2, n)),
            dma((2, n)),
            dma((2, n)),
            dma((2, n)),
        ],
        compiler_params=pltpu.CompilerParams(collective_id=1, has_side_effects=True),
        name="sum_grads",
    )(grad_a, grad_b)


def fast_shards(
    n,
    images_in,
    kernel,
    conv_bias,
    norm_gain,
    norm_shift,
    fp8_weight,
    block_scale,
    adapter_a,
    adapter_b,
    cotangent,
):
    weight = lax.all_gather(decode(fp8_weight, block_scale), "swap", axis=0, tiled=True)
    conv = exchange(n, images_in, kernel, conv_bias[:, None])
    grad_a, grad_b = main_part(
        conv, weight, cotangent, adapter_a, adapter_b, norm_gain, norm_shift
    )
    grad_a, grad_b = sum_all(n, grad_a, grad_b)
    return (grad_a.T, grad_b)


def fits(n, images_in, fp8_weight, adapter_a):
    channels, pixels = images_in.shape[1:]
    rank = adapter_a.shape[1]
    piece = pixels // n
    per = n // (rank // 8) if rank % 8 == 0 else 0
    wide = fp8_weight.shape[1]
    return (
        per > 0
        and n % (rank // 8) == 0
        and channels % CH == 0
        and pixels % SPAN == 0
        and SPAN % piece == 0
        and piece % 128 == 0
        and wide % 512 == 0
        and (channels * n) % (per * 128) == 0
        and wide % (per * 128) == 0
    )


def depthwise(images, kernel, conv_bias, map_width):
    batch, channels, pixels = images.shape
    maps = images.reshape(batch, channels, pixels // map_width, map_width)
    taps = kernel.reshape(channels, 1, KS, KS)
    half_span = KS // 2
    summed = lax.conv_general_dilated(
        maps,
        taps,
        (1, 1),
        ((half_span, half_span), (half_span, half_span)),
        dimension_numbers=("NCHW", "OIHW", "NCHW"),
        feature_group_count=channels,
        preferred_element_type=jnp.float32,
    )
    summed = summed.reshape(batch, channels, pixels)
    return summed + conv_bias[None, :, None]


def plain_shards(
    images_in,
    kernel,
    conv_bias,
    norm_gain,
    norm_shift,
    fp8_weight,
    block_scale,
    adapter_a,
    adapter_b,
    cotangent,
):
    conv = depthwise(images_in, kernel, conv_bias, W).astype(jnp.bfloat16)
    values = lax.all_to_all(conv, "swap", split_axis=2, concat_axis=1, tiled=True).astype(
        jnp.float32
    )
    average = jnp.mean(values, axis=1, keepdims=True)
    centred = values - average
    variance = jnp.mean(centred * centred, axis=1, keepdims=True)
    scaled = (
        centred * lax.rsqrt(variance + norm_eps) * norm_gain[None, :, None]
        + norm_shift[None, :, None]
    )
    normed = jnp.swapaxes(scaled, 1, 2).astype(jnp.bfloat16)
    own_rows = normed.reshape(-1, normed.shape[2])
    tokens = lax.all_gather(own_rows, "image", axis=0, tiled=True)
    zero_start = jnp.zeros((tokens.shape[0], fp8_weight.shape[1]), jnp.float32)
    local_weight = decode(fp8_weight, block_scale)
    shard_rows = lax.all_gather(local_weight, "swap", axis=0, tiled=True)
    columns = lax.slice_in_dim(tokens, 0, shard_rows.shape[0], axis=1)
    frozen = zero_start + jnp.dot(columns, shard_rows, preferred_element_type=jnp.float32)
    low_rank = jnp.dot(tokens, adapter_a, preferred_element_type=jnp.float32).astype(jnp.bfloat16)
    pre_act = frozen + adapter_scale * jnp.dot(
        low_rank, adapter_b, preferred_element_type=jnp.float32
    )
    upstream = cotangent.reshape(-1, cotangent.shape[2])
    grad_pre = (upstream.astype(jnp.float32) * gelu_slope(pre_act)).astype(jnp.bfloat16)
    grad_b_local = adapter_scale * jnp.dot(low_rank.T, grad_pre, preferred_element_type=jnp.float32)
    partial_back = jnp.dot(grad_pre, adapter_b.T, preferred_element_type=jnp.float32)
    contract = (((0,), (0,)), ((), ()))
    tokens_wide = tokens.astype(jnp.float32)
    summed_back = lax.psum(partial_back, "image")
    grad_a_local = adapter_scale * lax.dot_general(
        tokens_wide,
        summed_back,
        contract,
        precision=lax.Precision.HIGHEST,
        preferred_element_type=jnp.float32,
    )
    grad_a, grad_b = lax.psum((grad_a_local, grad_b_local), "swap")
    return (grad_a, grad_b)


def solution(mesh):
    placed = (
        P(("group", "image"), "swap", None),
        P("swap", None),
        P("swap"),
        P(),
        P(),
        P("swap", "image"),
        P("swap", "image"),
        P(),
        P(None, "image"),
        P("group", "swap", "image"),
    )
    n = mesh.shape["swap"]

    def shards(*arrays):
        if mesh.shape["image"] == 2 and fits(n, arrays[0], arrays[5], arrays[7]):
            return fast_shards(n, *arrays)
        return plain_shards(*arrays)

    return jax.shard_map(
        shards,
        mesh=mesh,
        in_specs=placed,
        out_specs=(P("group", None), P("group", "image")),
        check_vma=False,
    )
```

```python
import functools

import jax
import jax.numpy as jnp
from jax import lax
from jax.experimental import pallas as pl
from jax.experimental.pallas import tpu as pltpu
from jax.sharding import PartitionSpec as P

KS = 7
W = 64
HALF = KS // 2
MESH = pl.DeviceIdType.MESH
CH = 16
SPAN = 1024
MARGIN = 256


adapter_scale = 2.0
norm_eps = 1e-06


def power_table(scales):
    factor = jnp.zeros(scales.shape, jnp.float32)
    for exponent in range(-12, 4):
        factor = factor + jnp.where(
            scales == exponent, jnp.float32(2.0**exponent), jnp.float32(0.0)
        )
    return factor


def decode(weight, scales):
    row_count = weight.shape[0]
    groups = scales.shape[1]
    blocks = (
        weight.reshape(row_count, groups, -1).astype(jnp.float32) * power_table(scales)[:, :, None]
    )
    return blocks.reshape(row_count, -1).astype(jnp.bfloat16)


def gelu_slope(pre_act):
    cumulative = 0.5 * (1.0 + lax.erf(pre_act * 0.7071067811865476))
    density = jnp.exp(-0.5 * pre_act * pre_act) * 0.3989422804014327
    return cumulative + pre_act * density


def conv_block(x_ref, k_ref, b_ref, block, shifted, taps, put):
    pixels = x_ref.shape[-1]
    rows = pl.ds(pl.multiple_of(block * CH, CH), CH)
    x = x_ref[rows, :].astype(jnp.float32)
    column = lax.broadcasted_iota(jnp.int32, (CH, pixels), 1) & (W - 1)
    for b in range(KS):
        step = b - HALF
        if step == 0:
            moved = x
        else:
            moved = pltpu.roll(x, (-step) % pixels, axis=1)
            inside = column + step
            moved = jnp.where((inside >= 0) & (inside < W), moved, 0.0)
        shifted[b, :, MARGIN : MARGIN + pixels] = moved
    k = k_ref[rows, :].astype(jnp.float32)
    for t in range(KS * KS):
        taps[t] = jnp.broadcast_to(k[:, t : t + 1], (CH, 128))
    bias = b_ref[rows, :]

    def part(i, carry):
        start = i * SPAN
        even = jnp.broadcast_to(bias, (CH, SPAN))
        odd = jnp.zeros((CH, SPAN + 128), jnp.float32)
        for a in range(KS):
            step = a - HALF
            for b in range(KS):
                tap = taps[a * KS + b]
                if step % 2 == 0:
                    at = pl.ds(pl.multiple_of(start + MARGIN + step * W, 128), SPAN)
                    even = even + shifted[b, :, at] * jnp.tile(tap, (1, SPAN // 128))
                else:
                    at = pl.ds(pl.multiple_of(start + MARGIN + (step - 1) * W, 128), SPAN + 128)
                    odd = odd + shifted[b, :, at] * jnp.tile(tap, (1, SPAN // 128 + 1))
        moved = pltpu.roll(odd, SPAN + 128 - W, axis=1)[:, :SPAN]
        put(i, (even + moved).astype(jnp.bfloat16))
        return carry

    lax.fori_loop(0, pixels // SPAN, part, 0)


def exchange_kernel(
    n,
    x_hbm,
    k_ref,
    b_ref,
    w_hbm,
    out_hbm,
    w_out,
    x_buf,
    shifted,
    taps,
    stage,
    load_sem,
    own_sem,
    send_sem,
    recv_sem,
    fsend_sem,
    frecv_sem,
    w_own_sem,
    chain_send,
    chain_recv,
    side_send,
    side_recv,
):
    images, channels, pixels = x_hbm.shape
    piece = pixels // n
    me = lax.axis_index("swap")
    core = lax.axis_index("image")
    other = 1 - core
    first = core * images
    for i in range(images):
        pltpu.make_async_copy(x_hbm.at[i], x_buf.at[i], load_sem.at[i]).start()
    barrier = pltpu.get_barrier_semaphore()
    for k in range(1, n):
        pl.semaphore_signal(
            barrier, inc=1, device_id={"swap": lax.rem(me + k, n)}, device_id_type=MESH
        )
    pl.semaphore_signal(barrier, inc=1, device_id={"image": other}, device_id_type=MESH)
    shifted[...] = jnp.zeros_like(shifted)
    pl.semaphore_wait(barrier, n)

    my_rows = pl.ds(pl.multiple_of(me * channels, channels), channels)

    def sent(i, k):
        peer = lax.rem(me + k, n)
        return pltpu.make_async_remote_copy(
            src_ref=stage.at[i, peer],
            dst_ref=out_hbm.at[first + i, my_rows],
            send_sem=send_sem.at[i, k],
            recv_sem=recv_sem.at[i, k],
            device_id={"swap": peer},
            device_id_type=MESH,
        )

    def own(i):
        return pltpu.make_async_copy(
            stage.at[i, me], out_hbm.at[first + i, my_rows], own_sem.at[i]
        )

    def forward(i):
        return pltpu.make_async_remote_copy(
            src_ref=out_hbm.at[first + i],
            dst_ref=out_hbm.at[first + i],
            send_sem=fsend_sem.at[i],
            recv_sem=frecv_sem.at[i],
            device_id={"image": other},
            device_id_type=MESH,
        )

    depth = w_hbm.shape[0]
    line = n // 2
    spot = me // 2
    beside = me + 1 - 2 * lax.rem(me, 2)

    def w_rows(block):
        return w_out.at[pl.ds(pl.multiple_of(block * depth, depth), depth)]

    def w_move(src, block, peer, ss, rs):
        return pltpu.make_async_remote_copy(
            src_ref=src,
            dst_ref=w_rows(block),
            send_sem=ss,
            recv_sem=rs,
            device_id={"swap": peer},
            device_id_type=MESH,
        )

    def chain(way, s):
        block = me - way * 2 * (s - 1)
        src = w_hbm if s == 1 else w_rows(block)
        d = (1 - way) // 2
        return w_move(src, block, me + way * 2, chain_send.at[d, s], chain_recv.at[d, s])

    def comes(way, s):
        d = (1 - way) // 2
        block = me - way * 2 * s
        return w_move(w_rows(block), block, beside, chain_send.at[d, s], chain_recv.at[d, s])

    def side(way, s):
        block = me - way * 2 * s
        src = w_hbm if s == 0 else w_rows(block)
        d = (1 - way) // 2
        return w_move(src, block, beside, side_send.at[d, s], side_recv.at[d, s])

    def side_comes(way, s):
        d = (1 - way) // 2
        block = beside - way * 2 * s
        return w_move(w_rows(block), block, beside, side_send.at[d, s], side_recv.at[d, s])

    def held(way, s):
        place = spot - way * s
        return (place >= 0) & (place < line)

    def sends(way, s):
        return held(way, s - 1) & held(way, -1)

    def relay(s):
        for way in (1, -1):

            @pl.when(held(way, s))
            def _():
                comes(way, s).wait_recv()
                side(way, s).start()

            if s + 1 < line:

                @pl.when(sends(way, s + 1))
                def _():
                    chain(way, s + 1).start()

    def w_own():
        return pltpu.make_async_copy(w_hbm, w_rows(me), w_own_sem)

    for way in (1, -1):

        @pl.when(sends(way, 1))
        def _():
            chain(way, 1).start()

    side(1, 0).start()
    w_own().start()
    relayed = 1

    for i in range(images):
        pltpu.make_async_copy(x_hbm.at[i], x_buf.at[i], load_sem.at[i]).wait()

        def one(block, carry):
            rows = pl.ds(pl.multiple_of(block * CH, CH), CH)

            def put(j, values):
                for s in range(SPAN // piece):
                    stage[i, j * (SPAN // piece) + s, rows, :] = values[
                        :, s * piece : (s + 1) * piece
                    ]

            conv_block(x_buf.at[i], k_ref, b_ref, block, shifted, taps, put)
            return carry

        lax.fori_loop(0, channels // CH, one, 0)
        for k in range(1, n):
            sent(i, k).start()
        own(i).start()
        if i % 2 == 1 and relayed < line:
            relay(relayed)
            relayed += 1
    for s in range(relayed, line):
        relay(s)
    for i in range(images):
        for k in range(1, n):
            sent(i, k).wait_recv()
        own(i).wait()
        forward(i).start()
    for i in range(images):
        forward(i).wait_recv()
    for i in range(images):
        for k in range(1, n):
            sent(i, k).wait_send()
        forward(i).wait_send()
    w_own().wait()
    side_comes(1, 0).wait_recv()
    side(1, 0).wait_send()
    for s in range(1, line):
        for way in (1, -1):

            @pl.when(held(way, s))
            def _():
                side_comes(way, s).wait_recv()
                side(way, s).wait_send()

            @pl.when(sends(way, s))
            def _():
                chain(way, s).wait_send()


def exchange(n, images_in, kernel, conv_bias, weight):
    images, channels, pixels = images_in.shape
    piece = pixels // n
    dma = pltpu.SemaphoreType.DMA
    return pl.pallas_call(
        functools.partial(exchange_kernel, n),
        out_shape=(
            jax.ShapeDtypeStruct((2 * images, channels * n, piece), jnp.bfloat16),
            jax.ShapeDtypeStruct((weight.shape[0] * n, weight.shape[1]), jnp.bfloat16),
        ),
        in_specs=[
            pl.BlockSpec(memory_space=pltpu.HBM),
            pl.BlockSpec(memory_space=pltpu.VMEM),
            pl.BlockSpec(memory_space=pltpu.VMEM),
            pl.BlockSpec(memory_space=pltpu.HBM),
        ],
        out_specs=(
            pl.BlockSpec(memory_space=pltpu.HBM),
            pl.BlockSpec(memory_space=pltpu.HBM),
        ),
        scratch_shapes=[
            pltpu.VMEM((images, channels, pixels), jnp.bfloat16),
            pltpu.VMEM((KS, CH, pixels + 2 * MARGIN), jnp.float32),
            pltpu.VMEM((KS * KS, CH, 128), jnp.float32),
            pltpu.VMEM((images, n, channels, piece), jnp.bfloat16),
            dma((images,)),
            dma((images,)),
            dma((images, n)),
            dma((images, n)),
            dma((images,)),
            dma((images,)),
            dma,
            dma((2, n // 2)),
            dma((2, n // 2)),
            dma((2, n // 2)),
            dma((2, n // 2)),
        ],
        compiler_params=pltpu.CompilerParams(
            collective_id=0, has_side_effects=True, vmem_limit_bytes=48 * 2**20
        ),
        cost_estimate=pl.CostEstimate(
            flops=int(2e11), bytes_accessed=int(4e7), transcendentals=0
        ),
        name="conv_exchange",
    )(images_in, kernel, conv_bias, weight)


def main_kernel(x_ref, w_ref, cot_ref, a_ref, b_ref, gain_ref, shift_ref, ga_ref, gb_ref, tok):
    @pl.when(pl.program_id(0) == 0)
    def _():
        ga_ref[...] = jnp.zeros_like(ga_ref)
        gb_ref[...] = jnp.zeros_like(gb_ref)

    channels, piece = x_ref.shape[1:]
    hidden = w_ref.shape[1]
    lanes = 128
    for s in range(piece // lanes):
        at = slice(s * lanes, (s + 1) * lanes)
        x = x_ref[0, :, at].astype(jnp.float32)
        average = jnp.sum(x, axis=0, keepdims=True) * (1.0 / channels)
        centred = x - average
        variance = jnp.sum(centred * centred, axis=0, keepdims=True) * (1.0 / channels)
        scaled = centred * lax.rsqrt(variance + norm_eps) * gain_ref[...] + shift_ref[...]
        tok[at, :] = jnp.swapaxes(scaled, 0, 1).astype(jnp.bfloat16)
    tokens = tok[...]
    low = jnp.dot(tokens, a_ref[...], preferred_element_type=jnp.float32).astype(jnp.bfloat16)
    low_t = jnp.swapaxes(low.astype(jnp.float32), 0, 1).astype(jnp.bfloat16)
    step = 512

    def columns(j, back):
        at = pl.ds(pl.multiple_of(j * step, step), step)
        up = b_ref[:, at]
        pre = jnp.dot(tokens, w_ref[:, at], preferred_element_type=jnp.float32)
        pre = pre + adapter_scale * jnp.dot(low, up, preferred_element_type=jnp.float32)
        grad = (cot_ref[0, :, at].astype(jnp.float32) * gelu_slope(pre)).astype(jnp.bfloat16)
        gb_ref[:, at] += adapter_scale * jnp.dot(low_t, grad, preferred_element_type=jnp.float32)
        return back + lax.dot_general(
            up, grad, (((1,), (1,)), ((), ())), preferred_element_type=jnp.float32
        )

    back = jnp.zeros((b_ref.shape[0], piece), jnp.float32)
    for j in range(hidden // step):
        back = columns(j, back)
    high = back.astype(jnp.bfloat16)
    rest = back - high.astype(jnp.float32)
    middle = rest.astype(jnp.bfloat16)
    least = (rest - middle.astype(jnp.float32)).astype(jnp.bfloat16)
    total = jnp.dot(high, tokens, preferred_element_type=jnp.float32)
    total = total + jnp.dot(middle, tokens, preferred_element_type=jnp.float32)
    total = total + jnp.dot(least, tokens, preferred_element_type=jnp.float32)
    ga_ref[...] += adapter_scale * total


def main_part(conv, weight, cotangent, adapter_a, adapter_b, gain, shift):
    images, channels, piece = conv.shape
    hidden = weight.shape[1]
    rank = adapter_a.shape[1]
    once = lambda shape: pl.BlockSpec(
        shape, lambda i: (0,) * len(shape), pipeline_mode=pl.Buffered(1)
    )
    return pl.pallas_call(
        main_kernel,
        grid=(images,),
        out_shape=(
            jax.ShapeDtypeStruct((rank, channels), jnp.float32),
            jax.ShapeDtypeStruct((rank, hidden), jnp.float32),
        ),
        in_specs=[
            pl.BlockSpec((1, channels, piece), lambda i: (i, 0, 0)),
            once((channels, hidden)),
            pl.BlockSpec((1, piece, hidden), lambda i: (i, 0, 0)),
            once((channels, rank)),
            once((rank, hidden)),
            once((channels, 1)),
            once((channels, 1)),
        ],
        out_specs=(
            pl.BlockSpec((rank, channels), lambda i: (0, 0)),
            pl.BlockSpec((rank, hidden), lambda i: (0, 0)),
        ),
        scratch_shapes=[pltpu.VMEM((piece, channels), jnp.bfloat16)],
        compiler_params=pltpu.CompilerParams(
            dimension_semantics=("arbitrary",), vmem_limit_bytes=56 * 2**20
        ),
        cost_estimate=pl.CostEstimate(
            flops=int(4.4e10), bytes_accessed=int(5e7), transcendentals=int(2.5e7)
        ),
        name="tokens_main",
    )(conv, weight, cotangent, adapter_a, adapter_b, gain[:, None], shift[:, None])


def sum_kernel(n, ga_ref, gb_ref, oa_ref, ob_ref, pair, held, parts, total, pair_sem, s1, r1, s2, r2):
    me = lax.axis_index("swap")
    other = 1 - lax.axis_index("image")
    rank, wide_a = ga_ref.shape
    wide_b = gb_ref.shape[1]
    per = n // (rank // 8)
    ca, cb = wide_a // per, wide_b // per
    barrier = pltpu.get_barrier_semaphore()
    for k in range(1, n):
        pl.semaphore_signal(
            barrier, inc=1, device_id={"swap": lax.rem(me + k, n)}, device_id_type=MESH
        )
    pl.semaphore_signal(barrier, inc=1, device_id={"image": other}, device_id_type=MESH)
    pl.semaphore_wait(barrier, n)
    swap_a = pltpu.make_async_remote_copy(
        src_ref=ga_ref,
        dst_ref=pair,
        send_sem=pair_sem.at[0],
        recv_sem=pair_sem.at[1],
        device_id={"image": other},
        device_id_type=MESH,
    )
    swap_a.start()

    def place(ref, j, width):
        return ref.at[
            pl.ds(pl.multiple_of((j // per) * 8, 8), 8),
            pl.ds(pl.multiple_of((j % per) * width, 128), width),
        ]

    def move(src, dst, peer, ss, rs):
        return pltpu.make_async_remote_copy(
            src_ref=src,
            dst_ref=dst,
            send_sem=ss,
            recv_sem=rs,
            device_id={"swap": peer},
            device_id_type=MESH,
        )

    def scatter_b(k):
        peer = lax.rem(me + k, n)
        return move(
            place(gb_ref, peer, cb), parts.at[k, :, ca : ca + cb], peer, s1.at[1, k], r1.at[1, k]
        )

    def scatter_a(k):
        peer = lax.rem(me + k, n)
        return move(
            place(held, peer, ca), parts.at[k, :, 0:ca], peer, s1.at[0, k], r1.at[0, k]
        )

    for k in range(1, n):
        scatter_b(k).start()
    swap_a.wait()
    held[...] = ga_ref[...] + pair[...]
    for k in range(1, n):
        scatter_a(k).start()
    sum_b = place(gb_ref, me, cb)[...]
    for k in range(1, n):
        scatter_b(k).wait_recv()
        sum_b = sum_b + parts[k, :, ca : ca + cb]
    sum_a = place(held, me, ca)[...]
    for k in range(1, n):
        scatter_a(k).wait_recv()
        sum_a = sum_a + parts[k, :, 0:ca]
    total[:, 0:ca] = sum_a
    total[:, ca : ca + cb] = sum_b
    place(oa_ref, me, ca)[...] = sum_a
    place(ob_ref, me, cb)[...] = sum_b

    def gather_a(k):
        peer = lax.rem(me + k, n)
        return move(total.at[:, 0:ca], place(oa_ref, me, ca), peer, s2.at[0, k], r2.at[0, k])

    def gather_b(k):
        peer = lax.rem(me + k, n)
        return move(
            total.at[:, ca : ca + cb], place(ob_ref, me, cb), peer, s2.at[1, k], r2.at[1, k]
        )

    for k in range(1, n):
        gather_b(k).start()
        gather_a(k).start()
    for k in range(1, n):
        gather_b(k).wait_recv()
        gather_a(k).wait_recv()
    for k in range(1, n):
        scatter_a(k).wait_send()
        scatter_b(k).wait_send()
        gather_a(k).wait_send()
        gather_b(k).wait_send()


def sum_all(n, grad_a, grad_b):
    rank, wide_a = grad_a.shape
    wide_b = grad_b.shape[1]
    per = n // (rank // 8)
    wide = wide_a // per + wide_b // per
    dma = pltpu.SemaphoreType.DMA
    vmem = pl.BlockSpec(memory_space=pltpu.VMEM)
    return pl.pallas_call(
        functools.partial(sum_kernel, n),
        out_shape=(
            jax.ShapeDtypeStruct(grad_a.shape, jnp.float32),
            jax.ShapeDtypeStruct(grad_b.shape, jnp.float32),
        ),
        in_specs=[vmem, vmem],
        out_specs=(vmem, vmem),
        scratch_shapes=[
            pltpu.VMEM(grad_a.shape, jnp.float32),
            pltpu.VMEM(grad_a.shape, jnp.float32),
            pltpu.VMEM((n, 8, wide), jnp.float32),
            pltpu.VMEM((8, wide), jnp.float32),
            dma((2,)),
            dma((2, n)),
            dma((2, n)),
            dma((2, n)),
            dma((2, n)),
        ],
        compiler_params=pltpu.CompilerParams(collective_id=1, has_side_effects=True),
        name="sum_grads",
    )(grad_a, grad_b)


def fast_shards(
    n,
    images_in,
    kernel,
    conv_bias,
    norm_gain,
    norm_shift,
    fp8_weight,
    block_scale,
    adapter_a,
    adapter_b,
    cotangent,
):
    conv, weight = exchange(
        n, images_in, kernel, conv_bias[:, None], decode(fp8_weight, block_scale)
    )
    grad_a, grad_b = main_part(
        conv, weight, cotangent, adapter_a, adapter_b, norm_gain, norm_shift
    )
    grad_a, grad_b = sum_all(n, grad_a, grad_b)
    return (grad_a.T, grad_b)


def fits(n, images_in, fp8_weight, adapter_a):
    channels, pixels = images_in.shape[1:]
    rank = adapter_a.shape[1]
    piece = pixels // n
    per = n // (rank // 8) if rank % 8 == 0 else 0
    wide = fp8_weight.shape[1]
    return (
        per > 0
        and n % 2 == 0
        and n % (rank // 8) == 0
        and channels % CH == 0
        and pixels % SPAN == 0
        and SPAN % piece == 0
        and piece % 128 == 0
        and wide % 512 == 0
        and (channels * n) % (per * 128) == 0
        and wide % (per * 128) == 0
    )


def depthwise(images, kernel, conv_bias, map_width):
    batch, channels, pixels = images.shape
    maps = images.reshape(batch, channels, pixels // map_width, map_width)
    taps = kernel.reshape(channels, 1, KS, KS)
    half_span = KS // 2
    summed = lax.conv_general_dilated(
        maps,
        taps,
        (1, 1),
        ((half_span, half_span), (half_span, half_span)),
        dimension_numbers=("NCHW", "OIHW", "NCHW"),
        feature_group_count=channels,
        preferred_element_type=jnp.float32,
    )
    summed = summed.reshape(batch, channels, pixels)
    return summed + conv_bias[None, :, None]


def plain_shards(
    images_in,
    kernel,
    conv_bias,
    norm_gain,
    norm_shift,
    fp8_weight,
    block_scale,
    adapter_a,
    adapter_b,
    cotangent,
):
    conv = depthwise(images_in, kernel, conv_bias, W).astype(jnp.bfloat16)
    values = lax.all_to_all(conv, "swap", split_axis=2, concat_axis=1, tiled=True).astype(
        jnp.float32
    )
    average = jnp.mean(values, axis=1, keepdims=True)
    centred = values - average
    variance = jnp.mean(centred * centred, axis=1, keepdims=True)
    scaled = (
        centred * lax.rsqrt(variance + norm_eps) * norm_gain[None, :, None]
        + norm_shift[None, :, None]
    )
    normed = jnp.swapaxes(scaled, 1, 2).astype(jnp.bfloat16)
    own_rows = normed.reshape(-1, normed.shape[2])
    tokens = lax.all_gather(own_rows, "image", axis=0, tiled=True)
    zero_start = jnp.zeros((tokens.shape[0], fp8_weight.shape[1]), jnp.float32)
    local_weight = decode(fp8_weight, block_scale)
    shard_rows = lax.all_gather(local_weight, "swap", axis=0, tiled=True)
    columns = lax.slice_in_dim(tokens, 0, shard_rows.shape[0], axis=1)
    frozen = zero_start + jnp.dot(columns, shard_rows, preferred_element_type=jnp.float32)
    low_rank = jnp.dot(tokens, adapter_a, preferred_element_type=jnp.float32).astype(jnp.bfloat16)
    pre_act = frozen + adapter_scale * jnp.dot(
        low_rank, adapter_b, preferred_element_type=jnp.float32
    )
    upstream = cotangent.reshape(-1, cotangent.shape[2])
    grad_pre = (upstream.astype(jnp.float32) * gelu_slope(pre_act)).astype(jnp.bfloat16)
    grad_b_local = adapter_scale * jnp.dot(low_rank.T, grad_pre, preferred_element_type=jnp.float32)
    partial_back = jnp.dot(grad_pre, adapter_b.T, preferred_element_type=jnp.float32)
    contract = (((0,), (0,)), ((), ()))
    tokens_wide = tokens.astype(jnp.float32)
    summed_back = lax.psum(partial_back, "image")
    grad_a_local = adapter_scale * lax.dot_general(
        tokens_wide,
        summed_back,
        contract,
        precision=lax.Precision.HIGHEST,
        preferred_element_type=jnp.float32,
    )
    grad_a, grad_b = lax.psum((grad_a_local, grad_b_local), "swap")
    return (grad_a, grad_b)


def solution(mesh):
    placed = (
        P(("group", "image"), "swap", None),
        P("swap", None),
        P("swap"),
        P(),
        P(),
        P("swap", "image"),
        P("swap", "image"),
        P(),
        P(None, "image"),
        P("group", "swap", "image"),
    )
    n = mesh.shape["swap"]

    def shards(*arrays):
        if mesh.shape["image"] == 2 and fits(n, arrays[0], arrays[5], arrays[7]):
            return fast_shards(n, *arrays)
        return plain_shards(*arrays)

    return jax.shard_map(
        shards,
        mesh=mesh,
        in_specs=placed,
        out_specs=(P("group", None), P("group", "image")),
        check_vma=False,
    )
```
